256 devices in a mesh: seq: 64 (over y, x_hi, z), head: 4 (over x_lo, core).
Axes of the slice: x: 4 (x_hi: 2, x_lo: 2; x = x_hi * 2 + x_lo), y: 4, z: 8, core: 2. Of those that a mesh axis runs over, the one named last changes fastest.
Arguments:
- queries: bfloat16 [10240, 2560], P('seq', 'head'), may hold values from -48 to 48
- keys: bfloat16 [10240, 2560], P('seq', 'head'), may hold values from -9.625 to 9.625
- values: bfloat16 [10240, 2560], P('seq', 'head'), may hold values from -6 to 6
- out_weight: bfloat16 [2560, 5120], P('head'), may hold values from -0.125 to 0.125
Outputs:
- mixed: bfloat16 [10240, 5120], P('seq', 'head')
The draws below stay inside these ranges and needn't reach their ends.
All inputs are finite; a program needn't handle non-finite values.
Results may differ from the reference program's by a relative error of at most 0.015.
Values may be sent and summed in bfloat16 or wider, within the bound.
A program may use at most 192 MiB of HBM per device.

```python
import math
import jax
import jax.numpy as jnp
from jax import lax

D = 5120
HD = 128
HEADS = 20
TOK_DEV = 160
TOKENS = 10240
N_SEQ = 64


def draw_pair(key):
    base = jax.random.fold_in(key, 7101)
    key_query, key_key, key_order = jax.random.split(base, 3)
    width = HEADS * HD
    order = jax.random.permutation(key_order, TOKENS)
    query_field = 1.6 * jnp.clip(jax.random.normal(key_query, (TOKENS, width), jnp.float32), -6.0, 6.0)
    key_field = 1.6 * jnp.clip(jax.random.normal(key_key, (TOKENS, width), jnp.float32), -6.0, 6.0)
    query_field = query_field.at[order[48], 0].set(48.0).at[order[49], 1].set(-48.0)
    key_field = key_field.at[order[50], 0].set(9.625).at[order[51], 1].set(-9.625)
    return (query_field, key_field)


def draw_queries(key, part):
    return draw_pair(key)[0].astype(jnp.bfloat16)


def draw_keys(key, part):
    return draw_pair(key)[1].astype(jnp.bfloat16)


def block_levels(stream_key, shape, cuts, least, high):
    def one(position, blocks):
        draws = jax.random.uniform(jax.random.fold_in(jax.random.fold_in(stream_key, 6), position), (blocks,), jnp.float32, least / len(cuts), high / len(cuts))
        return jnp.repeat(jnp.exp(draws), shape[position] // blocks).reshape((-1,) + (1,) * (len(shape) - position - 1))

    level = one(*cuts[0])
    for cut in cuts[1:]:
        level = level * one(*cut)
    return level


def gaussian(stream_key, dims, scale, most, pieces=(), kind=jnp.bfloat16):
    values = scale * jax.random.normal(stream_key, dims, jnp.float32)
    if pieces:
        values = values * block_levels(stream_key, dims, pieces, -0.22, 0.18)
    return jnp.clip(values, -most, most).astype(kind)


def setup_inputs(seed: int = 0) -> dict:
    key_list = jax.random.split(jax.random.key(seed), 5)
    queries = draw_queries(jax.random.fold_in(key_list[4], 71), 0)
    keys = draw_keys(jax.random.fold_in(key_list[4], 71), 0)
    values = gaussian(key_list[2], (TOKENS, HEADS * HD), 1.0, 6.0, ((0, 64), (1, 4)))
    out_weight = gaussian(key_list[3], (HEADS * HD, D), (HEADS * HD) ** -0.5, 0.125, ((0, 4),))
    return {"queries": queries, "keys": keys, "values": values, "out_weight": out_weight}


def block_partial(query_all, key_block, value_block):
    scale = 1.0 / math.sqrt(HD)
    scores = jnp.einsum('thd,bhd->htb', query_all, key_block.astype(jnp.float32)) * scale
    block_max = lax.optimization_barrier(jnp.max(scores, axis=-1))
    expo = jnp.exp(scores - block_max[..., None])
    block_total = lax.optimization_barrier(jnp.sum(expo, axis=-1))
    weights = lax.optimization_barrier(expo.astype(jnp.bfloat16)).astype(jnp.float32)
    summed = jnp.einsum('htb,bhd->thd', weights, value_block.astype(jnp.float32))
    partial_value = summed / jnp.transpose(block_total)[..., None]
    partial_value = lax.optimization_barrier(partial_value.astype(jnp.bfloat16)).astype(jnp.float32)
    block_log = jnp.transpose(block_max + jnp.log(block_total))
    return (partial_value, block_log)

def reference(queries, keys, values, out_weight):
    width = HEADS * HD
    query_all = queries.astype(jnp.float32).reshape(TOKENS, HEADS, HD)
    key_blocks = keys.reshape(N_SEQ, TOK_DEV, HEADS, HD)
    value_blocks = values.reshape(N_SEQ, TOK_DEV, HEADS, HD)

    def absorb(state, blocks_in):
        key_block, value_block = blocks_in
        partial_value, block_log = block_partial(query_all, key_block, value_block)
        run_log, accum = state
        new_log = jnp.logaddexp(run_log, block_log)
        accum = accum * jnp.exp(run_log - new_log)[..., None] + partial_value * jnp.exp(block_log - new_log)[..., None]
        return ((new_log, accum), None)
    start_state = (jnp.full((TOKENS, HEADS), -1e+30, jnp.float32), jnp.zeros((TOKENS, HEADS, HD), jnp.float32))
    final_state, unused = lax.scan(absorb, start_state, (key_blocks, value_blocks))
    attended = final_state[1].astype(jnp.bfloat16).reshape(TOKENS, width)
    return jnp.dot(attended, out_weight, preferred_element_type=jnp.float32).astype(jnp.bfloat16)
```

```python
import functools
import math

import jax
import jax.numpy as jnp
from jax import lax
from jax.experimental import pallas as pl
from jax.experimental.pallas import tpu as pltpu
from jax.sharding import PartitionSpec as P

HD = 128
NY, NX, NZ, NXL, NC = 4, 2, 8, 2, 2
PARTS = 2
LOG2E = math.log2(math.e)


def position(slot):
    return (slot + 5) % NZ


class Copies:
    def __init__(self, send_sem, recv_sem):
        self.send_sem, self.recv_sem, self.made = send_sem, recv_sem, []

    def start(self, src, dst, device):
        n = len(self.made)
        copy = pltpu.make_async_remote_copy(
            src_ref=src,
            dst_ref=dst,
            send_sem=self.send_sem.at[n],
            recv_sem=self.recv_sem.at[n],
            device_id=device,
            device_id_type=pl.DeviceIdType.MESH,
        )
        copy.start()
        self.made.append(copy)
        return copy


def kernel(
    q_in, k_in, v_in, w_in, out_ref,
    q_all, k_all, v_all, w_all, acc, stat, part, part_stat, got, got_stat,
    term, core_got, far_got, mine, send_sem, recv_sem, local_sem,
):
    tok, width = q_in.shape
    heads = width // HD
    half = tok // PARTS
    cols = w_in.shape[1] // (NXL * NC)
    scale = LOG2E / math.sqrt(HD)
    copies = Copies(send_sem, recv_sem)

    seq, head = lax.axis_index("seq"), lax.axis_index("head")
    y, xh, z = seq // (NX * NZ), (seq // NZ) % NX, seq % NZ
    xl, core = head // NC, head % NC

    def at(y_, xh_, z_):
        return (y_ * (NX * NZ) + xh_ * NZ + z_, head)

    z_up, z_down = at(y, xh, (z + 1) % NZ), at(y, xh, (z + NZ - 1) % NZ)
    y_up, y_down = at((y + 1) % NY, xh, z), at((y + NY - 1) % NY, xh, z)
    x_far = at(y, 1 - xh, z)
    other_core = (seq, xl * NC + 1 - core)
    other_chip = (seq, (1 - xl) * NC + core)

    def q_rows(slot):
        return q_all.at[pl.ds(position(slot) * tok, tok), :]

    def rows(ref, far, place):
        return ref.at[far, pl.ds(place * tok, tok), :]

    own = [
        pltpu.make_async_copy(q_in, q_rows(0), local_sem.at[0]),
        pltpu.make_async_copy(k_in, rows(k_all, 0, 0), local_sem.at[1]),
        pltpu.make_async_copy(v_in, rows(v_all, 0, 0), local_sem.at[2]),
    ]
    weights = pltpu.make_async_copy(w_in, w_all, local_sem.at[3])
    for copy in own:
        copy.start()
    weights.start()

    partners = (z_up, z_down, y_up, y_down, x_far, other_core, other_chip)
    barrier = pltpu.get_barrier_semaphore()
    for partner in partners:
        pl.semaphore_signal(
            barrier, inc=1, device_id=partner, device_id_type=pl.DeviceIdType.MESH
        )
    stat[...] = jnp.zeros_like(stat)
    part_stat[...] = jnp.zeros_like(part_stat)
    pl.semaphore_wait(barrier, len(partners))

    up = copies.start(q_in, q_rows(7), z_up)
    down = copies.start(q_in, q_rows(1), z_down)
    k_up = copies.start(k_in, rows(k_all, 0, 3), y_up)
    v_down = copies.start(v_in, rows(v_all, 0, 1), y_down)
    v_up = copies.start(v_in, rows(v_all, 0, 3), y_up)
    k_down = copies.start(k_in, rows(k_all, 0, 1), y_down)
    k_far = copies.start(k_in, rows(k_all, 1, 0), x_far)
    v_far = copies.start(v_in, rows(v_all, 1, 0), x_far)

    up.wait_recv()
    up = copies.start(q_rows(7), q_rows(6), z_up)
    down.wait_recv()
    down = copies.start(q_rows(1), q_rows(2), z_down)
    k_up.wait_recv()
    k_fwd = copies.start(rows(k_all, 0, 3), rows(k_all, 0, 2), y_up)
    v_down.wait_recv()
    v_fwd = copies.start(rows(v_all, 0, 1), rows(v_all, 0, 2), y_down)
    up.wait_recv()
    up = copies.start(q_rows(6), q_rows(5), z_up)
    down.wait_recv()
    down = copies.start(q_rows(2), q_rows(3), z_down)
    k_far.wait_recv()
    k_up2 = copies.start(rows(k_all, 1, 0), rows(k_all, 1, 3), y_up)
    k_down2 = copies.start(rows(k_all, 1, 0), rows(k_all, 1, 1), y_down)
    v_far.wait_recv()
    v_down2 = copies.start(rows(v_all, 1, 0), rows(v_all, 1, 1), y_down)
    v_up2 = copies.start(rows(v_all, 1, 0), rows(v_all, 1, 3), y_up)
    up.wait_recv()
    up = copies.start(q_rows(5), q_rows(4), z_up)
    for copy in own:
        copy.wait()
    for copy in (v_up, k_down, k_fwd, v_fwd, down):
        copy.wait_recv()

    def attend(tile, far):
        here = slice(tile * 4 * tok, (tile + 1) * 4 * tok)
        for h in range(heads):
            hs = slice(h * HD, (h + 1) * HD)
            s = lax.dot_general(
                k_all[far, :, hs],
                q_all[here, hs],
                (((1,), (1,)), ((), ())),
                preferred_element_type=jnp.float32,
            )
            top = jnp.max(s, axis=0, keepdims=True) * scale
            if far:
                before = stat[h : h + 1, here]
                top = jnp.maximum(top, before)
            expo = jnp.exp2(s * scale - top)
            total = jnp.sum(expo, axis=0, keepdims=True)
            o = lax.dot_general(
                v_all[far, :, hs],
                expo.astype(jnp.bfloat16),
                (((0,), (0,)), ((), ())),
                preferred_element_type=jnp.float32,
            )
            if far:
                kept = jnp.exp2(before - top)
                total += kept * stat[8 + h : 9 + h, here]
                o += kept * acc[hs, here]
                part[here, hs] = jnp.transpose(o).astype(jnp.bfloat16)
            else:
                acc[hs, here] = o
            stat[h : h + 1, here] = top
            stat[8 + h : 9 + h, here] = total
        if far:
            both = stat[:, here]
            for n in range(4):
                for r in range(PARTS):
                    a = n * tok + r * half
                    part_stat[4 * tile + n, r, :, :half] = both[:, a : a + half]

    def part_rows(slot, r):
        return pl.ds(position(slot) * tok + r * half, half)

    def send_part(n, slot, r, device):
        o = copies.start(part.at[part_rows(slot, r), :], got.at[n, r], device)
        s = copies.start(part_stat.at[position(slot), r], got_stat.at[n, r], device)
        return (o, s)

    def merged(slot, r, arrivals, last):
        stats = [part_stat[position(slot), r]] + [got_stat[n, r] for n in arrivals]
        tops = [s[:8] for s in stats]
        top = functools.reduce(jnp.maximum, tops)
        shares = [jnp.exp2(t - top) for t in tops]
        total = sum(a * s[8:] for a, s in zip(shares, stats))
        if last:
            total = jnp.where(total == 0.0, 1.0, total)
            shares = [a / total for a in shares]
        blank = jnp.zeros((HD - 8 * len(shares), HD), jnp.float32)
        across = jnp.transpose(jnp.concatenate([*shares, blank], axis=0))
        values = [part[part_rows(slot, r), :]] + [got[n, r] for n in arrivals]
        outs = []
        for h in range(heads):
            hs = slice(h * HD, (h + 1) * HD)
            outs.append(
                sum(
                    v[:, hs].astype(jnp.float32) * across[:half, 8 * i + h : 8 * i + h + 1]
                    for i, v in enumerate(values)
                )
            )
        return jnp.concatenate(outs, axis=1).astype(jnp.bfloat16), top, total

    def pass_on(n, slot, r, arrival, device):
        o, top, total = merged(slot, r, (arrival,), False)
        part[part_rows(slot, r), :] = o
        part_stat[position(slot), r, :8] = top
        part_stat[position(slot), r, 8:] = total
        return send_part(n, slot, r, device)

    def arrive(pair):
        for copy in pair:
            copy.wait_recv()

    attend(1, 0)
    k_up2.wait_recv()
    k_fwd2 = copies.start(rows(k_all, 1, 3), rows(k_all, 1, 2), y_up)
    v_down2.wait_recv()
    v_fwd2 = copies.start(rows(v_all, 1, 1), rows(v_all, 1, 2), y_down)
    up.wait_recv()
    attend(0, 0)
    for copy in (k_down2, v_up2, k_fwd2, v_fwd2):
        copy.wait_recv()
    attend(0, 1)
    ups = [send_part(0, 4, r, z_up) for r in range(PARTS)]
    downs = [send_part(4, 5, r, z_down) for r in range(PARTS)]
    attend(1, 1)
    for step in (1, 2):
        for r in range(PARTS):
            arrive(ups[r])
            ups[r] = pass_on(step, 4 - step, r, step - 1, z_up)
            arrive(downs[r])
            downs[r] = pass_on(4 + step, 5 + step, r, 3 + step, z_down)
    for r in range(PARTS):
        arrive(ups[r])
        ups[r] = pass_on(3, 1, r, 2, z_up)

    weights.wait()

    def columns(j):
        return w_all[:, pl.ds(pl.multiple_of(j * cols, cols), cols)]

    far_here, far_there = (1 - xl) * NC + core, (1 - xl) * NC + 1 - core
    near_here, near_there = head, xl * NC + 1 - core
    waits = []
    for r in range(PARTS):
        arrive(ups[r])
        arrive(downs[r])
        attended = merged(0, r, (3, 6), True)[0]

        def product(j):
            return jnp.dot(attended, columns(j), preferred_element_type=jnp.float32)

        term[r, 0] = product(far_there).astype(jnp.bfloat16)
        first = copies.start(term.at[r, 0], core_got.at[r, 0], other_core)
        far = product(far_here)
        first.wait_recv()
        term[r, 1] = (far + core_got[r, 0].astype(jnp.float32)).astype(jnp.bfloat16)
        second = copies.start(term.at[r, 1], far_got.at[r], other_chip)
        term[r, 2] = product(near_there).astype(jnp.bfloat16)
        third = copies.start(term.at[r, 2], core_got.at[r, 1], other_core)
        mine[r] = product(near_here)
        waits.append((second, third))
    for r, pair in enumerate(waits):
        arrive(pair)
        out_ref[r * half : (r + 1) * half, :] = (
            mine[r]
            + core_got[r, 1].astype(jnp.float32)
            + far_got[r].astype(jnp.float32)
        ).astype(jnp.bfloat16)
    for copy in copies.made:
        copy.wait_send()


def on_device(queries, keys, values, out_weight):
    tok, width = queries.shape
    depth = out_weight.shape[1]
    cols = depth // (NXL * NC)
    half = tok // PARTS
    bf16, f32 = jnp.bfloat16, jnp.float32
    anywhere = pl.BlockSpec(memory_space=pl.ANY)
    return pl.pallas_call(
        kernel,
        out_shape=jax.ShapeDtypeStruct((tok, cols), bf16),
        in_specs=[anywhere] * 4,
        out_specs=pl.BlockSpec(memory_space=pltpu.VMEM),
        scratch_shapes=[
            pltpu.VMEM((NZ * tok, width), bf16),
            pltpu.VMEM((NX, NY * tok, width), bf16),
            pltpu.VMEM((NX, NY * tok, width), bf16),
            pltpu.VMEM((width, depth), bf16),
            pltpu.VMEM((width, NZ * tok), f32),
            pltpu.VMEM((16, NZ * tok), f32),
            pltpu.VMEM((NZ * tok, width), bf16),
            pltpu.VMEM((NZ, PARTS, 16, HD), f32),
            pltpu.VMEM((NZ - 1, PARTS, half, width), bf16),
            pltpu.VMEM((NZ - 1, PARTS, 16, HD), f32),
            pltpu.VMEM((PARTS, 3, half, cols), bf16),
            pltpu.VMEM((PARTS, 2, half, cols), bf16),
            pltpu.VMEM((PARTS, half, cols), bf16),
            pltpu.VMEM((PARTS, half, cols), f32),
            pltpu.SemaphoreType.DMA((64,)),
            pltpu.SemaphoreType.DMA((64,)),
            pltpu.SemaphoreType.DMA((4,)),
        ],
        compiler_params=pltpu.CompilerParams(
            collective_id=0, has_side_effects=True, vmem_limit_bytes=56 << 20
        ),
    )(queries, keys, values, out_weight)


def solution(mesh):
    placed = (P("seq", "head"), P("seq", "head"), P("seq", "head"), P("head", None))
    return jax.shard_map(
        on_device, mesh=mesh, in_specs=placed, out_specs=P("seq", "head"), check_vma=False
    )
```

```python
import functools
import math

import jax
import jax.numpy as jnp
from jax import lax
from jax.experimental import pallas as pl
from jax.experimental.pallas import tpu as pltpu
from jax.sharding import PartitionSpec as P

HD = 128
NY, NX, NZ, NXL, NC = 4, 2, 8, 2, 2
PARTS = 2
A_HEADS = 3
ORDER = (0, 1, 7, 2, 6, 3, 5, 4)
LANES = 128
LOG2E = math.log2(math.e)
F32, BF16 = jnp.float32, jnp.bfloat16


class Copies:
    def __init__(self, send_sem, recv_sem):
        self.send_sem, self.recv_sem, self.made = send_sem, recv_sem, []

    def start(self, src, dst, device):
        n = len(self.made)
        copy = pltpu.make_async_remote_copy(
            src_ref=src,
            dst_ref=dst,
            send_sem=self.send_sem.at[n],
            recv_sem=self.recv_sem.at[n],
            device_id=device,
            device_id_type=pl.DeviceIdType.MESH,
        )
        copy.start()
        self.made.append(copy)
        return copy


def arrive(*given):
    for copy in given:
        copy.wait_recv()


def combine(stats, values, heads, last):
    tops = [s[:8] for s in stats]
    top = functools.reduce(jnp.maximum, tops)
    shares = [jnp.exp2(t - top) for t in tops]
    total = sum(a * s[8:] for a, s in zip(shares, stats))
    if last:
        total = jnp.where(total == 0.0, 1.0, total)
        shares = [a / total for a in shares]
    blank = jnp.zeros((HD - 8 * len(shares), HD), F32)
    across = jnp.transpose(jnp.concatenate([*shares, blank], axis=0))
    rows = values[0].shape[0]
    outs = []
    for h in range(heads):
        hs = slice(h * HD, (h + 1) * HD)
        outs.append(
            sum(
                v[:, hs].astype(F32) * across[:rows, 8 * i + h : 8 * i + h + 1]
                for i, v in enumerate(values)
            )
        )
    return jnp.concatenate(outs, axis=1).astype(BF16), jnp.concatenate([top, total], axis=0)


def kernel(
    q_in, k_in, v_in, w_in, out_ref,
    qa, ka, va, qb, kb, vb, w_all, acc, stat_a,
    part_a, pst_a, got_a, gst_a, part_b, pst_b, got_b, gst_b, got_x, gst_x,
    att, term, far_got, mine, send_sem, recv_sem, local_sem,
):
    half, width = q_in.shape[1:]
    tok = PARTS * half
    heads = width // HD
    a_width = A_HEADS * HD
    cols = w_in.shape[1] // (NXL * NC)
    tile = NZ * half
    scale = LOG2E / math.sqrt(HD)
    copies = Copies(send_sem, recv_sem)
    start = copies.start
    on_a, on_b = pl.ds(0, a_width), pl.ds(a_width, width - a_width)

    seq, head = lax.axis_index("seq"), lax.axis_index("head")
    y, xh, z = seq // (NX * NZ), (seq // NZ) % NX, seq % NZ
    xl, core = head // NC, head % NC

    def at(y_, xh_, z_):
        return (y_ * (NX * NZ) + xh_ * NZ + z_, head)

    z_up, z_down = at(y, xh, (z + 1) % NZ), at(y, xh, (z + NZ - 1) % NZ)
    y_up, y_down = at((y + 1) % NY, xh, z), at((y + NY - 1) % NY, xh, z)
    x_far = at(y, 1 - xh, z)
    other_core = (seq, xl * NC + 1 - core)
    other_chip = (seq, (1 - xl) * NC + core)

    def qa_rows(slot):
        return pl.ds(ORDER.index(slot) * half, half)

    def qa_at(slot):
        return qa.at[:, qa_rows(slot), :]

    def a_at(ref, far, step):
        return ref.at[far, pl.ds(step * tok, tok), :]

    def qb_rows(far, step):
        return pl.ds((far * NY + step) * half, half)

    def qb_at(far, step):
        return qb.at[:, qb_rows(far, step), :]

    def b_at(ref, slot):
        return ref.at[pl.ds(slot * tok, tok), :]

    own = [
        pltpu.make_async_copy(q_in.at[:, :, on_a], qa_at(0), local_sem.at[0]),
        pltpu.make_async_copy(k_in.at[:, on_a], a_at(ka, 0, 0), local_sem.at[1]),
        pltpu.make_async_copy(v_in.at[:, on_a], a_at(va, 0, 0), local_sem.at[2]),
        pltpu.make_async_copy(q_in.at[:, :, on_b], qb_at(0, 0), local_sem.at[3]),
        pltpu.make_async_copy(k_in.at[:, on_b], b_at(kb, 0), local_sem.at[4]),
        pltpu.make_async_copy(v_in.at[:, on_b], b_at(vb, 0), local_sem.at[5]),
    ]
    my_rows = pl.ds(pl.multiple_of(core * width, width), width)

    def w_columns(x, c):
        return w_in.at[:, pl.ds(pl.multiple_of((x * NC + c) * cols, cols), cols)]

    weights = [
        pltpu.make_async_copy(w_columns(x, core), w_all.at[x, my_rows, :], local_sem.at[6 + x])
        for x in range(NXL)
    ]
    for copy in own:
        copy.start()
    for copy in weights:
        copy.start()

    partners = (z_up, z_down, y_up, y_down, x_far, other_core, other_chip)
    barrier = pltpu.get_barrier_semaphore()
    for partner in partners:
        pl.semaphore_signal(
            barrier, inc=1, device_id=partner, device_id_type=pl.DeviceIdType.MESH
        )
    stat_a[...] = jnp.zeros_like(stat_a)
    pst_a[...] = jnp.zeros_like(pst_a)
    pst_b[...] = jnp.zeros_like(pst_b)
    for copy in own:
        copy.wait()
    pl.semaphore_wait(barrier, len(partners))

    def attend(q, k):
        s = lax.dot_general(k, q, (((1,), (1,)), ((), ())), preferred_element_type=F32)
        return s, jnp.max(s, axis=0, keepdims=True) * scale

    def weigh(s, top, v):
        expo = jnp.exp2(s * scale - top)
        o = lax.dot_general(
            v, expo.astype(BF16), (((0,), (0,)), ((), ())), preferred_element_type=F32
        )
        return jnp.sum(expo, axis=0, keepdims=True), o

    def attend_a(r, lo, hi, far):
        for a in range(lo, hi, LANES):
            here = slice(r * tile + a, r * tile + a + LANES)
            for h in range(A_HEADS):
                hs = slice(h * HD, (h + 1) * HD)
                s, top = attend(qa[r, a : a + LANES, hs], ka[far, :, hs])
                if far:
                    before = stat_a[h : h + 1, here]
                    top = jnp.maximum(top, before)
                total, o = weigh(s, top, va[far, :, hs])
                if far:
                    kept = jnp.exp2(before - top)
                    total += kept * stat_a[8 + h : 9 + h, here]
                    o += kept * acc[hs, here]
                    part_a[r, a : a + LANES, hs] = jnp.transpose(o).astype(BF16)
                else:
                    acc[hs, here] = o
                stat_a[h : h + 1, here] = top
                stat_a[8 + h : 9 + h, here] = total
        if far:
            both = stat_a[:, r * tile : (r + 1) * tile]
            for n, slot in enumerate(ORDER):
                pst_a[r, slot, :, :half] = both[:, n * half : (n + 1) * half]

    def attend_b(r, h):
        hs = slice(h * HD, (h + 1) * HD)
        s, top = attend(qb[r, :, hs], kb[:, hs])
        total, o = weigh(s, top, vb[:, hs])
        o = jnp.transpose(o).astype(BF16)
        for n in range(NX * NY):
            here = slice(n * half, (n + 1) * half)
            part_b[r, n // NY, n % NY, :, hs] = o[here, :]
            pst_b[r, n // NY, n % NY, h : h + 1, :half] = top[:, here]
            pst_b[r, n // NY, n % NY, 8 + h : 9 + h, :half] = total[:, here]

    def long_a(r, d):
        return (NZ - d) % NZ if r else d

    def short_a(r, d):
        return d if r else (NZ - d) % NZ

    def long_b(r, d):
        return (NY - d) % NY if r else d

    def send_a(n, r, slot, device):
        return (
            start(part_a.at[r, qa_rows(slot), :], got_a.at[r, n], device),
            start(pst_a.at[r, slot], gst_a.at[r, n], device),
        )

    def send_b(n, r, step, device):
        return (
            start(part_b.at[r, :, step], got_b.at[r, n], device),
            start(pst_b.at[r, :, step], gst_b.at[r, n], device),
        )

    def pass_on_a(n, r, slot, arrival, device):
        o, stat = combine(
            [pst_a[r, slot], gst_a[r, arrival]],
            [part_a[r, qa_rows(slot), :], got_a[r, arrival]],
            A_HEADS,
            False,
        )
        part_a[r, qa_rows(slot), :] = o
        pst_a[r, slot] = stat
        return send_a(n, r, slot, device)

    longs_a, shorts_a, longs_b, shorts_b, across_b = {}, {}, {}, {}, {}

    def ring(r, step):
        far, near = (z_down, z_up) if r else (z_up, z_down)
        if step:
            arrive(*longs_a[r])
            longs_a[r] = pass_on_a(step, r, long_a(r, 4 - step), step - 1, far)
            if step < 3:
                arrive(*shorts_a[r])
                shorts_a[r] = pass_on_a(4 + step, r, short_a(r, 3 - step), 3 + step, near)
        else:
            longs_a[r] = send_a(0, r, long_a(r, 4), far)
            shorts_a[r] = send_a(4, r, short_a(r, 3), near)

    def plane(r, step):
        far, near = (y_down, y_up) if r else (y_up, y_down)
        if step == 0:
            longs_b[r] = send_b(0, r, 2, far)
            shorts_b[r] = send_b(2, r, long_b(r, 3), near)
        elif step == 1:
            arrive(*longs_b[r])
            d = long_b(r, 1)
            for x in range(NX):
                o, stat = combine(
                    [pst_b[r, x, d], gst_b[r, 0, x]],
                    [part_b[r, x, d], got_b[r, 0, x]],
                    heads - A_HEADS,
                    False,
                )
                part_b[r, x, d] = o
                pst_b[r, x, d] = stat
            longs_b[r] = send_b(1, r, d, far)
        else:
            arrive(*longs_b[r], *shorts_b[r])
            o, stat = combine(
                [pst_b[r, 1, 0], gst_b[r, 1, 1], gst_b[r, 2, 1]],
                [part_b[r, 1, 0], got_b[r, 1, 1], got_b[r, 2, 1]],
                heads - A_HEADS,
                False,
            )
            part_b[r, 1, 0] = o
            pst_b[r, 1, 0] = stat
            across_b[r] = (
                start(part_b.at[r, 1, 0], got_x.at[r], x_far),
                start(pst_b.at[r, 1, 0], gst_x.at[r], x_far),
            )

    def attended(r):
        arrive(*longs_a[r], *shorts_a[r], *across_b[r])
        first = combine(
            [pst_a[r, 0], gst_a[r, 3], gst_a[r, 6]],
            [part_a[r, qa_rows(0), :], got_a[r, 3], got_a[r, 6]],
            A_HEADS,
            True,
        )[0]
        second = combine(
            [pst_b[r, 0, 0], gst_b[r, 1, 0], gst_b[r, 2, 0], gst_x[r]],
            [part_b[r, 0, 0], got_b[r, 1, 0], got_b[r, 2, 0], got_x[r]],
            heads - A_HEADS,
            True,
        )[0]
        return jnp.concatenate([first, second], axis=1)

    qa_u = start(qa_at(0), qa_at(7), z_up)
    qa_d = start(qa_at(0), qa_at(1), z_down)
    k_u = start(a_at(ka, 0, 0), a_at(ka, 0, 3), y_up)
    v_d = start(a_at(va, 0, 0), a_at(va, 0, 1), y_down)
    k_x = start(a_at(ka, 0, 0), a_at(ka, 1, 0), x_far)
    v_x = start(a_at(va, 0, 0), a_at(va, 1, 0), x_far)
    v_u = start(a_at(va, 0, 0), a_at(va, 0, 3), y_up)
    k_d = start(a_at(ka, 0, 0), a_at(ka, 0, 1), y_down)
    w_far = [
        start(w_columns(x, 1 - core), w_all.at[x, my_rows, :], other_core) for x in range(NXL)
    ]
    first = qa_u
    first.wait_send()
    kv_u = [start(b_at(ref, 0), b_at(ref, 7), z_up) for ref in (kb, vb)]
    kv_d = [start(b_at(ref, 0), b_at(ref, 1), z_down) for ref in (kb, vb)]

    arrive(qa_u)
    qa_u = start(qa_at(7), qa_at(6), z_up)
    arrive(qa_d)
    qa_d = start(qa_at(1), qa_at(2), z_down)
    arrive(k_u)
    k_f = start(a_at(ka, 0, 3), a_at(ka, 0, 2), y_up)
    arrive(v_d)
    v_f = start(a_at(va, 0, 1), a_at(va, 0, 2), y_down)
    arrive(k_x, v_x)
    far_a = [
        start(a_at(ref, 1, 0), a_at(ref, 1, step), device)
        for ref in (ka, va)
        for step, device in ((3, y_up), (1, y_down))
    ]
    qb_x = start(qb_at(0, 0), qb_at(1, 0), x_far)
    arrive(*kv_u)
    kv_u = [start(b_at(ref, 7), b_at(ref, 6), z_up) for ref in (kb, vb)]
    arrive(*kv_d)
    kv_d = [start(b_at(ref, 1), b_at(ref, 2), z_down) for ref in (kb, vb)]
    arrive(qa_u)
    qa_u = start(qa_at(6), qa_at(5), z_up)
    arrive(qa_d)
    qa_d = start(qa_at(2), qa_at(3), z_down)
    qb_u = start(qb_at(0, 0), qb_at(0, 3), y_up)
    qb_d = start(qb_at(0, 0), qb_at(0, 1), y_down)
    arrive(k_f, v_f)
    far_a += [start(a_at(ref, 0, 2), a_at(ref, 1, 2), x_far) for ref in (ka, va)]
    arrive(qb_x)
    far_b = [
        start(qb_at(1, 0), qb_at(1, step), device) for step, device in ((3, y_up), (1, y_down))
    ]
    arrive(v_u, k_d)

    attend_a(0, 0, 384, 0)
    attend_a(1, 0, 384, 0)
    arrive(*kv_u)
    kv_u = [start(b_at(ref, 6), b_at(ref, 5), z_up) for ref in (kb, vb)]
    arrive(*kv_d)
    kv_d = [start(b_at(ref, 2), b_at(ref, 3), z_down) for ref in (kb, vb)]
    arrive(qa_u)
    qa_u = start(qa.at[0, qa_rows(5), :], qa.at[0, qa_rows(4), :], z_up)
    arrive(qa_d)
    qa_d = start(qa.at[1, qa_rows(3), :], qa.at[1, qa_rows(4), :], z_down)
    attend_a(0, 384, 512, 0)
    attend_a(1, 384, 512, 0)
    arrive(qb_u, qb_d)
    qb_u = start(qb.at[0, qb_rows(0, 3), :], qb.at[0, qb_rows(0, 2), :], y_up)
    qb_d = start(qb.at[1, qb_rows(0, 1), :], qb.at[1, qb_rows(0, 2), :], y_down)
    arrive(qa_u, qa_d)
    attend_a(0, 512, tile, 0)
    attend_a(1, 512, tile, 0)
    arrive(*far_a)
    arrive(*kv_u)
    k_l = start(b_at(kb, 5), b_at(kb, 4), z_up)
    arrive(*kv_d)
    v_l = start(b_at(vb, 3), b_at(vb, 4), z_down)
    attend_a(0, 0, tile, 1)
    ring(0, 0)
    arrive(qb_u, qb_d)
    far_b.append(start(qb_at(0, 2), qb_at(1, 2), x_far))
    attend_a(1, 0, tile, 1)
    ring(1, 0)
    ring(0, 1)
    arrive(k_l, v_l, *far_b)
    attend_b(0, 0)
    ring(1, 1)
    attend_b(0, 1)
    plane(0, 0)
    ring(0, 2)
    attend_b(1, 0)
    attend_b(1, 1)
    plane(1, 0)
    ring(1, 2)
    ring(0, 3)
    plane(0, 1)
    ring(1, 3)
    plane(1, 1)
    plane(0, 2)
    plane(1, 2)

    for copy in weights:
        copy.wait()
    arrive(*w_far)

    def product(r, x):
        return sum(
            jnp.dot(
                att[r, c],
                w_all[x, c * width : (c + 1) * width, :],
                preferred_element_type=F32,
            )
            for c in range(NC)
        )

    swaps, sums = [], []
    for r in range(PARTS):
        att[r, core] = attended(r)
        swaps.append(start(att.at[r, core], att.at[r, core], other_core))
    for r in range(PARTS):
        arrive(swaps[r])
        term[r] = product(r, 1 - xl).astype(BF16)
        sums.append(start(term.at[r], far_got.at[r], other_chip))
    for r in range(PARTS):
        mine[r] = product(r, xl)
    for r in range(PARTS):
        arrive(sums[r])
        out_ref[r * half : (r + 1) * half, :] = (mine[r] + far_got[r].astype(F32)).astype(BF16)
    for copy in copies.made:
        if copy is not first:
            copy.wait_send()


def on_device(queries, keys, values, out_weight):
    tok, width = queries.shape
    depth = out_weight.shape[1]
    cols = depth // (NXL * NC)
    half = tok // PARTS
    a_width = A_HEADS * HD
    b_width = width - a_width
    anywhere = pl.BlockSpec(memory_space=pl.ANY)
    return pl.pallas_call(
        kernel,
        out_shape=jax.ShapeDtypeStruct((tok, cols), BF16),
        in_specs=[anywhere] * 4,
        out_specs=pl.BlockSpec(memory_space=pltpu.VMEM),
        scratch_shapes=[
            pltpu.VMEM((PARTS, NZ * half, a_width), BF16),
            pltpu.VMEM((NX, NY * tok, a_width), BF16),
            pltpu.VMEM((NX, NY * tok, a_width), BF16),
            pltpu.VMEM((PARTS, NX * NY * half, b_width), BF16),
            pltpu.VMEM((NZ * tok, b_width), BF16),
            pltpu.VMEM((NZ * tok, b_width), BF16),
            pltpu.VMEM((NXL, NC * width, cols), BF16),
            pltpu.VMEM((a_width, NZ * tok), F32),
            pltpu.VMEM((16, NZ * tok), F32),
            pltpu.VMEM((PARTS, NZ * half, a_width), BF16),
            pltpu.VMEM((PARTS, NZ, 16, HD), F32),
            pltpu.VMEM((PARTS, NZ - 1, half, a_width), BF16),
            pltpu.VMEM((PARTS, NZ - 1, 16, HD), F32),
            pltpu.VMEM((PARTS, NX, NY, half, b_width), BF16),
            pltpu.VMEM((PARTS, NX, NY, 16, HD), F32),
            pltpu.VMEM((PARTS, 3, NX, half, b_width), BF16),
            pltpu.VMEM((PARTS, 3, NX, 16, HD), F32),
            pltpu.VMEM((PARTS, half, b_width), BF16),
            pltpu.VMEM((PARTS, 16, HD), F32),
            pltpu.VMEM((PARTS, NC, half, width), BF16),
            pltpu.VMEM((PARTS, half, cols), BF16),
            pltpu.VMEM((PARTS, half, cols), BF16),
            pltpu.VMEM((PARTS, half, cols), F32),
            pltpu.SemaphoreType.DMA((96,)),
            pltpu.SemaphoreType.DMA((96,)),
            pltpu.SemaphoreType.DMA((8,)),
        ],
        compiler_params=pltpu.CompilerParams(
            collective_id=0, has_side_effects=True, vmem_limit_bytes=56 << 20
        ),
    )(queries.reshape(PARTS, half, width), keys, values, out_weight)


def solution(mesh):
    placed = (P("seq", "head"), P("seq", "head"), P("seq", "head"), P("head", None))
    return jax.shard_map(
        on_device, mesh=mesh, in_specs=placed, out_specs=P("seq", "head"), check_vma=False
    )
```

```python
import functools
import math

import jax
import jax.numpy as jnp
from jax import lax
from jax.experimental import pallas as pl
from jax.experimental.pallas import tpu as pltpu
from jax.sharding import PartitionSpec as P

HD = 128
NY, NX, NZ, NXL, NC = 4, 2, 8, 2, 2
PARTS = 2
A_HEADS = 3
ORDER = (0, 1, 7, 2, 6, 3, 5, 4)
LANES = 128
LOG2E = math.log2(math.e)
F32, BF16 = jnp.float32, jnp.bfloat16


class Copies:
    def __init__(self, send_sem, recv_sem):
        self.send_sem, self.recv_sem, self.made = send_sem, recv_sem, []

    def start(self, src, dst, device):
        n = len(self.made)
        copy = pltpu.make_async_remote_copy(
            src_ref=src,
            dst_ref=dst,
            send_sem=self.send_sem.at[n],
            recv_sem=self.recv_sem.at[n],
            device_id=device,
            device_id_type=pl.DeviceIdType.MESH,
        )
        copy.start()
        self.made.append(copy)
        return copy


def arrive(*given):
    for copy in given:
        copy.wait_recv()


def combine(stats, values, heads, last):
    tops = [s[:8] for s in stats]
    top = functools.reduce(jnp.maximum, tops)
    shares = [jnp.exp2(t - top) for t in tops]
    total = sum(a * s[8:] for a, s in zip(shares, stats))
    if last:
        total = jnp.where(total == 0.0, 1.0, total)
        shares = [a / total for a in shares]
    blank = jnp.zeros((HD - 8 * len(shares), HD), F32)
    across = jnp.transpose(jnp.concatenate([*shares, blank], axis=0))
    rows = values[0].shape[0]
    outs = []
    for h in range(heads):
        hs = slice(h * HD, (h + 1) * HD)
        outs.append(
            sum(
                v[:, hs].astype(F32) * across[:rows, 8 * i + h : 8 * i + h + 1]
                for i, v in enumerate(values)
            )
        )
    return jnp.concatenate(outs, axis=1).astype(BF16), jnp.concatenate([top, total], axis=0)


def kernel(
    q_in, k_in, v_in, w_in, out_ref,
    qa, ka, va, qb, kb, vb, w_all, acc, stat_a,
    part_a, pst_a, got_a, gst_a, part_b, pst_b, got_b, gst_b,
    att, term, far_got, mine, send_sem, recv_sem, local_sem,
):
    half, width = q_in.shape[1:]
    tok = PARTS * half
    heads = width // HD
    a_width = A_HEADS * HD
    cols = w_in.shape[1] // (NXL * NC)
    tile = NZ * half
    scale = LOG2E / math.sqrt(HD)
    copies = Copies(send_sem, recv_sem)
    start = copies.start
    on_a, on_b = pl.ds(0, a_width), pl.ds(a_width, width - a_width)

    seq, head = lax.axis_index("seq"), lax.axis_index("head")
    y, xh, z = seq // (NX * NZ), (seq // NZ) % NX, seq % NZ
    xl, core = head // NC, head % NC

    def at(y_, xh_, z_):
        return (y_ * (NX * NZ) + xh_ * NZ + z_, head)

    z_up, z_down = at(y, xh, (z + 1) % NZ), at(y, xh, (z + NZ - 1) % NZ)
    y_up, y_down = at((y + 1) % NY, xh, z), at((y + NY - 1) % NY, xh, z)
    x_far = at(y, 1 - xh, z)
    other_core = (seq, xl * NC + 1 - core)
    other_chip = (seq, (1 - xl) * NC + core)

    def qa_rows(slot):
        return pl.ds(ORDER.index(slot) * half, half)

    def qa_at(slot):
        return qa.at[:, qa_rows(slot), :]

    def a_at(ref, far, step):
        return ref.at[far, pl.ds(step * tok, tok), :]

    def qb_rows(far, step):
        return pl.ds((far * NY + step) * half, half)

    def qb_at(far, step):
        return qb.at[:, qb_rows(far, step), :]

    def b_at(ref, slot):
        return ref.at[pl.ds(slot * tok, tok), :]

    own = [
        pltpu.make_async_copy(q_in.at[:, :, on_a], qa_at(0), local_sem.at[0]),
        pltpu.make_async_copy(k_in.at[:, on_a], a_at(ka, 0, 0), local_sem.at[1]),
        pltpu.make_async_copy(v_in.at[:, on_a], a_at(va, 0, 0), local_sem.at[2]),
        pltpu.make_async_copy(q_in.at[:, :, on_b], qb_at(0, 0), local_sem.at[3]),
        pltpu.make_async_copy(k_in.at[:, on_b], b_at(kb, 0), local_sem.at[4]),
        pltpu.make_async_copy(v_in.at[:, on_b], b_at(vb, 0), local_sem.at[5]),
    ]
    my_rows = pl.ds(pl.multiple_of(core * width, width), width)

    def w_columns(x, c):
        return w_in.at[:, pl.ds(pl.multiple_of((x * NC + c) * cols, cols), cols)]

    weights = [
        pltpu.make_async_copy(w_columns(x, core), w_all.at[x, my_rows, :], local_sem.at[6 + x])
        for x in range(NXL)
    ]
    for copy in own:
        copy.start()
    for copy in weights:
        copy.start()

    partners = [z_up, z_down, other_core, other_chip]
    partners += [
        at((y + step) % NY, 1 - xh if x else xh, z)
        for x in range(NX)
        for step in range(NY)
        if x or step
    ]
    barrier = pltpu.get_barrier_semaphore()
    for partner in partners:
        pl.semaphore_signal(
            barrier, inc=1, device_id=partner, device_id_type=pl.DeviceIdType.MESH
        )
    stat_a[...] = jnp.zeros_like(stat_a)
    pst_a[...] = jnp.zeros_like(pst_a)
    pst_b[...] = jnp.zeros_like(pst_b)
    for copy in own:
        copy.wait()
    pl.semaphore_wait(barrier, len(partners))

    def attend(q, k):
        s = lax.dot_general(k, q, (((1,), (1,)), ((), ())), preferred_element_type=F32)
        return s, jnp.max(s, axis=0, keepdims=True) * scale

    def weigh(s, top, v):
        expo = jnp.exp2(s * scale - top)
        o = lax.dot_general(
            v, expo.astype(BF16), (((0,), (0,)), ((), ())), preferred_element_type=F32
        )
        return jnp.sum(expo, axis=0, keepdims=True), o

    def attend_a(r, lo, hi, far):
        for a in range(lo, hi, LANES):
            here = slice(r * tile + a, r * tile + a + LANES)
            for h in range(A_HEADS):
                hs = slice(h * HD, (h + 1) * HD)
                s, top = attend(qa[r, a : a + LANES, hs], ka[far, :, hs])
                if far:
                    before = stat_a[h : h + 1, here]
                    top = jnp.maximum(top, before)
                total, o = weigh(s, top, va[far, :, hs])
                if far:
                    kept = jnp.exp2(before - top)
                    total += kept * stat_a[8 + h : 9 + h, here]
                    o += kept * acc[hs, here]
                    part_a[r, a : a + LANES, hs] = jnp.transpose(o).astype(BF16)
                else:
                    acc[hs, here] = o
                stat_a[h : h + 1, here] = top
                stat_a[8 + h : 9 + h, here] = total
        if far:
            both = stat_a[:, r * tile : (r + 1) * tile]
            for n, slot in enumerate(ORDER):
                pst_a[r, slot, :, :half] = both[:, n * half : (n + 1) * half]

    def attend_b(r, h):
        hs = slice(h * HD, (h + 1) * HD)
        s, top = attend(qb[r, :, hs], kb[:, hs])
        total, o = weigh(s, top, vb[:, hs])
        o = jnp.transpose(o).astype(BF16)
        for n in range(NX * NY):
            here = slice(n * half, (n + 1) * half)
            part_b[r, n, :, hs] = o[here, :]
            pst_b[r, n, h : h + 1, :half] = top[:, here]
            pst_b[r, n, 8 + h : 9 + h, :half] = total[:, here]

    def long_a(r, d):
        return (NZ - d) % NZ if r else d

    def short_a(r, d):
        return d if r else (NZ - d) % NZ

    def send_a(n, r, slot, device):
        return (
            start(part_a.at[r, qa_rows(slot), :], got_a.at[r, n], device),
            start(pst_a.at[r, slot], gst_a.at[r, n], device),
        )

    def pass_on_a(n, r, slot, arrival, device):
        o, stat = combine(
            [pst_a[r, slot], gst_a[r, arrival]],
            [part_a[r, qa_rows(slot), :], got_a[r, arrival]],
            A_HEADS,
            False,
        )
        part_a[r, qa_rows(slot), :] = o
        pst_a[r, slot] = stat
        return send_a(n, r, slot, device)

    longs_a, shorts_a, spread_b = {}, {}, {}

    def ring(r, step):
        far, near = (z_down, z_up) if r else (z_up, z_down)
        if step:
            arrive(*longs_a[r])
            longs_a[r] = pass_on_a(step, r, long_a(r, 4 - step), step - 1, far)
            if step < 3:
                arrive(*shorts_a[r])
                shorts_a[r] = pass_on_a(4 + step, r, short_a(r, 3 - step), 3 + step, near)
        else:
            longs_a[r] = send_a(0, r, long_a(r, 4), far)
            shorts_a[r] = send_a(4, r, short_a(r, 3), near)

    def plane(r):
        spread_b[r] = []
        for step in (2, 1, 3, 0):
            for x in (1, 0):
                if x or step:
                    n = x * NY + step
                    owner = at((y + step) % NY, 1 - xh if x else xh, z)
                    spread_b[r] += [
                        start(part_b.at[r, n], got_b.at[r, n], owner),
                        start(pst_b.at[r, n], gst_b.at[r, n], owner),
                    ]

    def attended(r):
        arrive(*longs_a[r], *shorts_a[r], *spread_b[r])
        first = combine(
            [pst_a[r, 0], gst_a[r, 3], gst_a[r, 6]],
            [part_a[r, qa_rows(0), :], got_a[r, 3], got_a[r, 6]],
            A_HEADS,
            True,
        )[0]
        second = combine(
            [pst_b[r, 0]] + [gst_b[r, n] for n in range(1, NX * NY)],
            [part_b[r, 0]] + [got_b[r, n] for n in range(1, NX * NY)],
            heads - A_HEADS,
            True,
        )[0]
        return jnp.concatenate([first, second], axis=1)

    def q_piece(r):
        return lambda slot: qa.at[r, qa_rows(slot), :]

    def kv_piece(ref):
        return lambda slot: b_at(ref, slot)

    q_streams = [(q_piece(0), True), (q_piece(1), False)]
    kv_streams = [(kv_piece(kb), True), (kv_piece(vb), False)]
    moving = {}

    def z_first(streams):
        for piece, up in streams:
            moving[piece] = [start(piece(0), piece(7), z_up), start(piece(0), piece(1), z_down)]

    def z_on(streams, d):
        for piece, up in streams:
            came_up, came_down = moving[piece]
            arrive(came_up)
            nxt = []
            if d < 3 or up:
                nxt.append(start(piece(8 - d), piece(7 - d), z_up))
            arrive(came_down)
            if d < 3 or not up:
                nxt.append(start(piece(d), piece(d + 1), z_down))
            moving[piece] = nxt

    def z_last(streams):
        for piece, up in streams:
            arrive(*moving[piece])

    z_first(q_streams)
    k_u = start(a_at(ka, 0, 0), a_at(ka, 0, 3), y_up)
    v_d = start(a_at(va, 0, 0), a_at(va, 0, 1), y_down)
    k_x = start(a_at(ka, 0, 0), a_at(ka, 1, 0), x_far)
    v_x = start(a_at(va, 0, 0), a_at(va, 1, 0), x_far)
    v_u = start(a_at(va, 0, 0), a_at(va, 0, 3), y_up)
    k_d = start(a_at(ka, 0, 0), a_at(ka, 0, 1), y_down)
    w_far = [
        start(w_columns(x, 1 - core), w_all.at[x, my_rows, :], other_core) for x in range(NXL)
    ]
    z_on(q_streams, 1)
    z_first(kv_streams)
    arrive(k_u)
    k_f = start(a_at(ka, 0, 3), a_at(ka, 0, 2), y_up)
    arrive(v_d)
    v_f = start(a_at(va, 0, 1), a_at(va, 0, 2), y_down)
    far_a = []
    for came, ref in ((k_x, ka), (v_x, va)):
        arrive(came)
        far_a += [
            start(a_at(ref, 1, 0), a_at(ref, 1, step), device)
            for step, device in ((3, y_up), (1, y_down))
        ]
    qb_x = start(qb_at(0, 0), qb_at(1, 0), x_far)
    z_on(q_streams, 2)
    z_on(kv_streams, 1)
    qb_u = start(qb_at(0, 0), qb_at(0, 3), y_up)
    qb_d = start(qb_at(0, 0), qb_at(0, 1), y_down)
    for came, ref in ((k_f, ka), (v_f, va)):
        arrive(came)
        far_a.append(start(a_at(ref, 0, 2), a_at(ref, 1, 2), x_far))
    arrive(qb_x)
    far_b = [
        start(qb_at(1, 0), qb_at(1, step), device) for step, device in ((3, y_up), (1, y_down))
    ]
    arrive(v_u, k_d)

    attend_a(0, 0, 384, 0)
    z_on(q_streams, 3)
    attend_a(1, 0, 384, 0)
    z_on(kv_streams, 2)
    attend_a(0, 384, 512, 0)
    attend_a(1, 384, 512, 0)
    arrive(qb_u)
    qb_u = start(qb.at[0, qb_rows(0, 3), :], qb.at[0, qb_rows(0, 2), :], y_up)
    arrive(qb_d)
    qb_d = start(qb.at[1, qb_rows(0, 1), :], qb.at[1, qb_rows(0, 2), :], y_down)
    z_last(q_streams)
    attend_a(0, 512, tile, 0)
    attend_a(1, 512, tile, 0)
    arrive(*far_a)
    attend_a(0, 0, tile, 1)
    ring(0, 0)
    z_on(kv_streams, 3)
    arrive(qb_u, qb_d)
    far_b.append(start(qb_at(0, 2), qb_at(1, 2), x_far))
    attend_a(1, 0, tile, 1)
    ring(1, 0)
    ring(0, 1)
    z_last(kv_streams)
    arrive(*far_b)
    b_heads = heads - A_HEADS
    attend_b(0, 0)
    ring(1, 1)
    for h in range(1, b_heads):
        attend_b(0, h)
    plane(0)
    ring(0, 2)
    for h in range(b_heads):
        attend_b(1, h)
    plane(1)
    ring(1, 2)
    ring(0, 3)
    ring(1, 3)

    for copy in weights:
        copy.wait()
    arrive(*w_far)

    def product(r, x):
        return sum(
            jnp.dot(
                att[r, c],
                w_all[x, c * width : (c + 1) * width, :],
                preferred_element_type=F32,
            )
            for c in range(NC)
        )

    sums = []
    for r in range(PARTS):
        att[r, core] = attended(r)
        swap = start(att.at[r, core], att.at[r, core], other_core)
        if r:
            mine[r - 1] = product(r - 1, xl)
        arrive(swap)
        term[r] = product(r, 1 - xl).astype(BF16)
        sums.append(start(term.at[r], far_got.at[r], other_chip))
    mine[r] = product(r, xl)
    for r in range(PARTS):
        arrive(sums[r])
        out_ref[r * half : (r + 1) * half, :] = (mine[r] + far_got[r].astype(F32)).astype(BF16)
    for copy in copies.made:
        copy.wait_send()


def on_device(queries, keys, values, out_weight):
    tok, width = queries.shape
    depth = out_weight.shape[1]
    cols = depth // (NXL * NC)
    half = tok // PARTS
    a_width = A_HEADS * HD
    b_width = width - a_width
    anywhere = pl.BlockSpec(memory_space=pl.ANY)
    return pl.pallas_call(
        kernel,
        out_shape=jax.ShapeDtypeStruct((tok, cols), BF16),
        in_specs=[anywhere] * 4,
        out_specs=pl.BlockSpec(memory_space=pltpu.VMEM),
        scratch_shapes=[
            pltpu.VMEM((PARTS, NZ * half, a_width), BF16),
            pltpu.VMEM((NX, NY * tok, a_width), BF16),
            pltpu.VMEM((NX, NY * tok, a_width), BF16),
            pltpu.VMEM((PARTS, NX * NY * half, b_width), BF16),
            pltpu.VMEM((NZ * tok, b_width), BF16),
            pltpu.VMEM((NZ * tok, b_width), BF16),
            pltpu.VMEM((NXL, NC * width, cols), BF16),
            pltpu.VMEM((a_width, NZ * tok), F32),
            pltpu.VMEM((16, NZ * tok), F32),
            pltpu.VMEM((PARTS, NZ * half, a_width), BF16),
            pltpu.VMEM((PARTS, NZ, 16, HD), F32),
            pltpu.VMEM((PARTS, NZ - 1, half, a_width), BF16),
            pltpu.VMEM((PARTS, NZ - 1, 16, HD), F32),
            pltpu.VMEM((PARTS, NX * NY, half, b_width), BF16),
            pltpu.VMEM((PARTS, NX * NY, 16, HD), F32),
            pltpu.VMEM((PARTS, NX * NY, half, b_width), BF16),
            pltpu.VMEM((PARTS, NX * NY, 16, HD), F32),
            pltpu.VMEM((PARTS, NC, half, width), BF16),
            pltpu.VMEM((PARTS, half, cols), BF16),
            pltpu.VMEM((PARTS, half, cols), BF16),
            pltpu.VMEM((PARTS, half, cols), F32),
            pltpu.SemaphoreType.DMA((128,)),
            pltpu.SemaphoreType.DMA((128,)),
            pltpu.SemaphoreType.DMA((8,)),
        ],
        compiler_params=pltpu.CompilerParams(
            collective_id=0, has_side_effects=True, vmem_limit_bytes=56 << 20
        ),
    )(queries.reshape(PARTS, half, width), keys, values, out_weight)


def solution(mesh):
    placed = (P("seq", "head"), P("seq", "head"), P("seq", "head"), P("head", None))
    return jax.shard_map(
        on_device, mesh=mesh, in_specs=placed, out_specs=P("seq", "head"), check_vma=False
    )
```

```python
import functools
import math

import jax
import jax.numpy as jnp
from jax import lax
from jax.experimental import pallas as pl
from jax.experimental.pallas import tpu as pltpu
from jax.sharding import PartitionSpec as P

HD = 128
NY, NX, NZ, NXL, NC = 4, 2, 8, 2, 2
PARTS = 2
A_HEADS = 3
ORDER = (0, 1, 7, 2, 6, 3, 5, 4)
LANES = 128
LOG2E = math.log2(math.e)
F32, BF16 = jnp.float32, jnp.bfloat16


class Copies:
    def __init__(self, send_sem, recv_sem):
        self.send_sem, self.recv_sem, self.made = send_sem, recv_sem, []

    def start(self, src, dst, device):
        n = len(self.made)
        copy = pltpu.make_async_remote_copy(
            src_ref=src,
            dst_ref=dst,
            send_sem=self.send_sem.at[n],
            recv_sem=self.recv_sem.at[n],
            device_id=device,
            device_id_type=pl.DeviceIdType.MESH,
        )
        copy.start()
        self.made.append(copy)
        return copy


def arrive(*given):
    for copy in given:
        copy.wait_recv()


def combine(stats, values, heads, last):
    tops = [s[:8] for s in stats]
    top = functools.reduce(jnp.maximum, tops)
    shares = [jnp.exp2(t - top) for t in tops]
    total = sum(a * s[8:] for a, s in zip(shares, stats))
    if last:
        total = jnp.where(total == 0.0, 1.0, total)
        shares = [a / total for a in shares]
    blank = jnp.zeros((HD - 8 * len(shares), HD), F32)
    across = jnp.transpose(jnp.concatenate([*shares, blank], axis=0))
    rows = values[0].shape[0]
    outs = []
    for h in range(heads):
        hs = slice(h * HD, (h + 1) * HD)
        outs.append(
            sum(
                v[:, hs].astype(F32) * across[:rows, 8 * i + h : 8 * i + h + 1]
                for i, v in enumerate(values)
            )
        )
    return jnp.concatenate(outs, axis=1).astype(BF16), jnp.concatenate([top, total], axis=0)


def kernel(
    q_in, k_in, v_in, w_in, out_ref,
    qa, ka, va, qb, kb, vb, w_all, acc, stat_a,
    part_a, pst_a, got_a, gst_a, part_b, pst_b, got_b, gst_b,
    att, term, far_got, mine, send_sem, recv_sem, local_sem,
):
    half, width = q_in.shape[1:]
    tok = PARTS * half
    heads = width // HD
    a_width = A_HEADS * HD
    cols = w_in.shape[1] // (NXL * NC)
    tile = NZ * half
    scale = LOG2E / math.sqrt(HD)
    copies = Copies(send_sem, recv_sem)
    start = copies.start
    on_a, on_b = pl.ds(0, a_width), pl.ds(a_width, width - a_width)

    seq, head = lax.axis_index("seq"), lax.axis_index("head")
    y, xh, z = seq // (NX * NZ), (seq // NZ) % NX, seq % NZ
    xl, core = head // NC, head % NC

    def at(y_, xh_, z_):
        return (y_ * (NX * NZ) + xh_ * NZ + z_, head)

    z_up, z_down = at(y, xh, (z + 1) % NZ), at(y, xh, (z + NZ - 1) % NZ)
    z_up2, z_down2 = at(y, xh, (z + 2) % NZ), at(y, xh, (z + NZ - 2) % NZ)
    y_up, y_down = at((y + 1) % NY, xh, z), at((y + NY - 1) % NY, xh, z)
    x_far = at(y, 1 - xh, z)
    other_core = (seq, xl * NC + 1 - core)
    other_chip = (seq, (1 - xl) * NC + core)

    def qa_rows(slot):
        return pl.ds(ORDER.index(slot) * half, half)

    def qa_at(slot):
        return qa.at[:, qa_rows(slot), :]

    def a_at(ref, far, step):
        return ref.at[far, pl.ds(step * tok, tok), :]

    def qb_rows(far, step):
        return pl.ds((far * NY + step) * half, half)

    def qb_at(far, step):
        return qb.at[:, qb_rows(far, step), :]

    def b_at(ref, slot):
        return ref.at[pl.ds(slot * tok, tok), :]

    own = [
        pltpu.make_async_copy(q_in.at[:, :, on_a], qa_at(0), local_sem.at[0]),
        pltpu.make_async_copy(k_in.at[:, on_a], a_at(ka, 0, 0), local_sem.at[1]),
        pltpu.make_async_copy(v_in.at[:, on_a], a_at(va, 0, 0), local_sem.at[2]),
        pltpu.make_async_copy(q_in.at[:, :, on_b], qb_at(0, 0), local_sem.at[3]),
        pltpu.make_async_copy(k_in.at[:, on_b], b_at(kb, 0), local_sem.at[4]),
        pltpu.make_async_copy(v_in.at[:, on_b], b_at(vb, 0), local_sem.at[5]),
    ]
    my_rows = pl.ds(pl.multiple_of(core * width, width), width)

    def w_columns(x, c):
        return w_in.at[:, pl.ds(pl.multiple_of((x * NC + c) * cols, cols), cols)]

    weights = [
        pltpu.make_async_copy(w_columns(x, core), w_all.at[x, my_rows, :], local_sem.at[6 + x])
        for x in range(NXL)
    ]
    for copy in own:
        copy.start()
    for copy in weights:
        copy.start()

    partners = [z_up, z_down, z_up2, z_down2, other_core, other_chip]
    partners += [
        at((y + step) % NY, 1 - xh if x else xh, z)
        for x in range(NX)
        for step in range(NY)
        if x or step
    ]
    barrier = pltpu.get_barrier_semaphore()
    for partner in partners:
        pl.semaphore_signal(
            barrier, inc=1, device_id=partner, device_id_type=pl.DeviceIdType.MESH
        )
    stat_a[...] = jnp.zeros_like(stat_a)
    pst_a[...] = jnp.zeros_like(pst_a)
    pst_b[...] = jnp.zeros_like(pst_b)
    for copy in own:
        copy.wait()
    pl.semaphore_wait(barrier, len(partners))

    def attend(q, k):
        s = lax.dot_general(k, q, (((1,), (1,)), ((), ())), preferred_element_type=F32)
        return s, jnp.max(s, axis=0, keepdims=True) * scale

    def weigh(s, top, v):
        expo = jnp.exp2(s * scale - top)
        o = lax.dot_general(
            v, expo.astype(BF16), (((0,), (0,)), ((), ())), preferred_element_type=F32
        )
        return jnp.sum(expo, axis=0, keepdims=True), o

    def attend_a(r, lo, hi, far):
        for a in range(lo, hi, LANES):
            here = slice(r * tile + a, r * tile + a + LANES)
            for h in range(A_HEADS):
                hs = slice(h * HD, (h + 1) * HD)
                s, top = attend(qa[r, a : a + LANES, hs], ka[far, :, hs])
                if far:
                    before = stat_a[h : h + 1, here]
                    top = jnp.maximum(top, before)
                total, o = weigh(s, top, va[far, :, hs])
                if far:
                    kept = jnp.exp2(before - top)
                    total += kept * stat_a[8 + h : 9 + h, here]
                    o += kept * acc[hs, here]
                    part_a[r, a : a + LANES, hs] = jnp.transpose(o).astype(BF16)
                else:
                    acc[hs, here] = o
                stat_a[h : h + 1, here] = top
                stat_a[8 + h : 9 + h, here] = total
        if far:
            both = stat_a[:, r * tile : (r + 1) * tile]
            for n, slot in enumerate(ORDER):
                pst_a[r, slot, :, :half] = both[:, n * half : (n + 1) * half]

    def attend_b(r, h):
        hs = slice(h * HD, (h + 1) * HD)
        s, top = attend(qb[r, :, hs], kb[:, hs])
        total, o = weigh(s, top, vb[:, hs])
        o = jnp.transpose(o).astype(BF16)
        for n in range(NX * NY):
            here = slice(n * half, (n + 1) * half)
            part_b[r, n, :, hs] = o[here, :]
            pst_b[r, n, h : h + 1, :half] = top[:, here]
            pst_b[r, n, 8 + h : 9 + h, :half] = total[:, here]

    def long_a(r, d):
        return (NZ - d) % NZ if r else d

    def short_a(r, d):
        return d if r else (NZ - d) % NZ

    def send_a(n, r, slot, device):
        return (
            start(part_a.at[r, qa_rows(slot), :], got_a.at[r, n], device),
            start(pst_a.at[r, slot], gst_a.at[r, n], device),
        )

    def pass_on_a(n, r, slot, arrivals, device):
        o, stat = combine(
            [pst_a[r, slot]] + [gst_a[r, m] for m in arrivals],
            [part_a[r, qa_rows(slot), :]] + [got_a[r, m] for m in arrivals],
            A_HEADS,
            False,
        )
        part_a[r, qa_rows(slot), :] = o
        pst_a[r, slot] = stat
        return send_a(n, r, slot, device)

    longs_a, shorts_a, ends_a, spread_b = {}, {}, {}, {}

    def ring(r, step):
        far, near = (z_down, z_up) if r else (z_up, z_down)
        far2, near2 = (z_down2, z_up2) if r else (z_up2, z_down2)
        if step == 0:
            longs_a[r] = send_a(0, r, long_a(r, 4), far2) + send_a(1, r, long_a(r, 3), far)
            shorts_a[r] = send_a(2, r, short_a(r, 3), near)
            ends_a[r] = send_a(3, r, long_a(r, 1), far) + send_a(4, r, short_a(r, 1), near)
        else:
            arrive(*longs_a[r])
            longs_a[r] = pass_on_a(5, r, long_a(r, 2), (0, 1), far2)
            arrive(*shorts_a[r])
            shorts_a[r] = pass_on_a(6, r, short_a(r, 2), (2,), near2)

    def plane(r):
        spread_b[r] = []
        for step in (2, 1, 3, 0):
            for x in (1, 0):
                if x or step:
                    n = x * NY + step
                    owner = at((y + step) % NY, 1 - xh if x else xh, z)
                    spread_b[r] += [
                        start(part_b.at[r, n], got_b.at[r, n], owner),
                        start(pst_b.at[r, n], gst_b.at[r, n], owner),
                    ]

    def attended(r):
        arrive(*longs_a[r], *shorts_a[r], *ends_a[r], *spread_b[r])
        first = combine(
            [pst_a[r, 0]] + [gst_a[r, n] for n in range(3, 7)],
            [part_a[r, qa_rows(0), :]] + [got_a[r, n] for n in range(3, 7)],
            A_HEADS,
            True,
        )[0]
        second = combine(
            [pst_b[r, 0]] + [gst_b[r, n] for n in range(1, NX * NY)],
            [part_b[r, 0]] + [got_b[r, n] for n in range(1, NX * NY)],
            heads - A_HEADS,
            True,
        )[0]
        return jnp.concatenate([first, second], axis=1)

    def q_piece(r):
        return lambda slot: qa.at[r, qa_rows(slot), :]

    def kv_piece(ref):
        return lambda slot: b_at(ref, slot)

    q_streams = [(q_piece(0), True), (q_piece(1), False)]
    kv_streams = [(kv_piece(kb), True), (kv_piece(vb), False)]
    moving = {}

    def z_first(streams):
        for piece, up in streams:
            moving[piece] = [start(piece(0), piece(7), z_up), start(piece(0), piece(1), z_down)]

    def z_on(streams, d):
        for piece, up in streams:
            came_up, came_down = moving[piece]
            arrive(came_up)
            nxt = []
            if d < 3 or up:
                nxt.append(start(piece(8 - d), piece(7 - d), z_up))
            arrive(came_down)
            if d < 3 or not up:
                nxt.append(start(piece(d), piece(d + 1), z_down))
            moving[piece] = nxt

    def z_last(streams):
        for piece, up in streams:
            arrive(*moving[piece])

    z_first(q_streams)
    k_u = start(a_at(ka, 0, 0), a_at(ka, 0, 3), y_up)
    v_d = start(a_at(va, 0, 0), a_at(va, 0, 1), y_down)
    k_x = start(a_at(ka, 0, 0), a_at(ka, 1, 0), x_far)
    v_x = start(a_at(va, 0, 0), a_at(va, 1, 0), x_far)
    v_u = start(a_at(va, 0, 0), a_at(va, 0, 3), y_up)
    k_d = start(a_at(ka, 0, 0), a_at(ka, 0, 1), y_down)
    w_far = [
        start(w_columns(x, 1 - core), w_all.at[x, my_rows, :], other_core) for x in range(NXL)
    ]
    z_on(q_streams, 1)
    z_first(kv_streams)
    arrive(k_u)
    k_f = start(a_at(ka, 0, 3), a_at(ka, 0, 2), y_up)
    arrive(v_d)
    v_f = start(a_at(va, 0, 1), a_at(va, 0, 2), y_down)
    far_a = []
    for came, ref in ((k_x, ka), (v_x, va)):
        arrive(came)
        far_a += [
            start(a_at(ref, 1, 0), a_at(ref, 1, step), device)
            for step, device in ((3, y_up), (1, y_down))
        ]
    qb_x = start(qb_at(0, 0), qb_at(1, 0), x_far)
    z_on(q_streams, 2)
    z_on(kv_streams, 1)
    qb_u = start(qb_at(0, 0), qb_at(0, 3), y_up)
    qb_d = start(qb_at(0, 0), qb_at(0, 1), y_down)
    for came, ref in ((k_f, ka), (v_f, va)):
        arrive(came)
        far_a.append(start(a_at(ref, 0, 2), a_at(ref, 1, 2), x_far))
    arrive(qb_x)
    far_b = [
        start(qb_at(1, 0), qb_at(1, step), device) for step, device in ((3, y_up), (1, y_down))
    ]
    arrive(v_u, k_d)

    attend_a(0, 0, 384, 0)
    z_on(q_streams, 3)
    attend_a(1, 0, 384, 0)
    z_on(kv_streams, 2)
    attend_a(0, 384, 512, 0)
    attend_a(1, 384, 512, 0)
    arrive(qb_u)
    qb_u = start(qb.at[0, qb_rows(0, 3), :], qb.at[0, qb_rows(0, 2), :], y_up)
    arrive(qb_d)
    qb_d = start(qb.at[1, qb_rows(0, 1), :], qb.at[1, qb_rows(0, 2), :], y_down)
    z_last(q_streams)
    attend_a(0, 512, tile, 0)
    attend_a(1, 512, tile, 0)
    arrive(*far_a)
    z_on(kv_streams, 3)
    arrive(qb_u, qb_d)
    far_b.append(start(qb_at(0, 2), qb_at(1, 2), x_far))
    attend_a(0, 0, tile, 1)
    ring(0, 0)
    attend_a(1, 0, tile, 1)
    ring(1, 0)
    z_last(kv_streams)
    arrive(*far_b)
    for h in range(heads - A_HEADS):
        attend_b(0, h)
    plane(0)
    ring(0, 1)
    for h in range(heads - A_HEADS):
        attend_b(1, h)
    plane(1)
    ring(1, 1)

    for copy in weights:
        copy.wait()
    arrive(*w_far)

    def product(r, x):
        return sum(
            jnp.dot(
                att[r, c],
                w_all[x, c * width : (c + 1) * width, :],
                preferred_element_type=F32,
            )
            for c in range(NC)
        )

    sums = []
    for r in range(PARTS):
        att[r, core] = attended(r)
        swap = start(att.at[r, core], att.at[r, core], other_core)
        if r:
            mine[r - 1] = product(r - 1, xl)
        arrive(swap)
        term[r] = product(r, 1 - xl).astype(BF16)
        sums.append(start(term.at[r], far_got.at[r], other_chip))
    mine[r] = product(r, xl)
    for r in range(PARTS):
        arrive(sums[r])
        out_ref[r * half : (r + 1) * half, :] = (mine[r] + far_got[r].astype(F32)).astype(BF16)
    for copy in copies.made:
        copy.wait_send()


def on_device(queries, keys, values, out_weight):
    tok, width = queries.shape
    depth = out_weight.shape[1]
    cols = depth // (NXL * NC)
    half = tok // PARTS
    a_width = A_HEADS * HD
    b_width = width - a_width
    anywhere = pl.BlockSpec(memory_space=pl.ANY)
    return pl.pallas_call(
        kernel,
        out_shape=jax.ShapeDtypeStruct((tok, cols), BF16),
        in_specs=[anywhere] * 4,
        out_specs=pl.BlockSpec(memory_space=pltpu.VMEM),
        scratch_shapes=[
            pltpu.VMEM((PARTS, NZ * half, a_width), BF16),
            pltpu.VMEM((NX, NY * tok, a_width), BF16),
            pltpu.VMEM((NX, NY * tok, a_width), BF16),
            pltpu.VMEM((PARTS, NX * NY * half, b_width), BF16),
            pltpu.VMEM((NZ * tok, b_width), BF16),
            pltpu.VMEM((NZ * tok, b_width), BF16),
            pltpu.VMEM((NXL, NC * width, cols), BF16),
            pltpu.VMEM((a_width, NZ * tok), F32),
            pltpu.VMEM((16, NZ * tok), F32),
            pltpu.VMEM((PARTS, NZ * half, a_width), BF16),
            pltpu.VMEM((PARTS, NZ, 16, HD), F32),
            pltpu.VMEM((PARTS, NZ - 1, half, a_width), BF16),
            pltpu.VMEM((PARTS, NZ - 1, 16, HD), F32),
            pltpu.VMEM((PARTS, NX * NY, half, b_width), BF16),
            pltpu.VMEM((PARTS, NX * NY, 16, HD), F32),
            pltpu.VMEM((PARTS, NX * NY, half, b_width), BF16),
            pltpu.VMEM((PARTS, NX * NY, 16, HD), F32),
            pltpu.VMEM((PARTS, NC, half, width), BF16),
            pltpu.VMEM((PARTS, half, cols), BF16),
            pltpu.VMEM((PARTS, half, cols), BF16),
            pltpu.VMEM((PARTS, half, cols), F32),
            pltpu.SemaphoreType.DMA((128,)),
            pltpu.SemaphoreType.DMA((128,)),
            pltpu.SemaphoreType.DMA((8,)),
        ],
        compiler_params=pltpu.CompilerParams(
            collective_id=0, has_side_effects=True, vmem_limit_bytes=56 << 20
        ),
    )(queries.reshape(PARTS, half, width), keys, values, out_weight)


def solution(mesh):
    placed = (P("seq", "head"), P("seq", "head"), P("seq", "head"), P("head", None))
    return jax.shard_map(
        on_device, mesh=mesh, in_specs=placed, out_specs=P("seq", "head"), check_vma=False
    )
```

```python
import functools
import math

import jax
import jax.numpy as jnp
from jax import lax
from jax.experimental import pallas as pl
from jax.experimental.pallas import tpu as pltpu
from jax.sharding import PartitionSpec as P

HD = 128
NY, NX, NZ, NXL, NC = 4, 2, 8, 2, 2
PARTS = 2
A_HEADS = 3
ORDER = (0, 1, 7, 2, 6, 3, 5, 4)
LANES = 128
LOG2E = math.log2(math.e)
F32, BF16 = jnp.float32, jnp.bfloat16


class Copies:
    def __init__(self, send_sem, recv_sem):
        self.send_sem, self.recv_sem, self.made = send_sem, recv_sem, []

    def start(self, src, dst, device):
        n = len(self.made)
        copy = pltpu.make_async_remote_copy(
            src_ref=src,
            dst_ref=dst,
            send_sem=self.send_sem.at[n],
            recv_sem=self.recv_sem.at[n],
            device_id=device,
            device_id_type=pl.DeviceIdType.MESH,
        )
        copy.start()
        self.made.append(copy)
        return copy


def arrive(*given):
    for copy in given:
        copy.wait_recv()


def combine(stats, values, heads, last):
    tops = [s[:8] for s in stats]
    top = functools.reduce(jnp.maximum, tops)
    shares = [jnp.exp2(t - top) for t in tops]
    total = sum(a * s[8:] for a, s in zip(shares, stats))
    if last:
        total = jnp.where(total == 0.0, 1.0, total)
        shares = [a / total for a in shares]
    blank = jnp.zeros((HD - 8 * len(shares), HD), F32)
    across = jnp.transpose(jnp.concatenate([*shares, blank], axis=0))
    rows = values[0].shape[0]
    outs = []
    for h in range(heads):
        hs = slice(h * HD, (h + 1) * HD)
        outs.append(
            sum(
                v[:, hs].astype(F32) * across[:rows, 8 * i + h : 8 * i + h + 1]
                for i, v in enumerate(values)
            )
        )
    return jnp.concatenate(outs, axis=1).astype(BF16), jnp.concatenate([top, total], axis=0)


def kernel(
    q_in, k_in, v_in, w_in, out_ref,
    qa, ka, va, qb, kb, vb, w_all, acc, stat_a,
    part_a, pst_a, got_a, gst_a, part_b, pst_b, got_b, gst_b,
    att, term, far_got, mine, send_sem, recv_sem, local_sem,
):
    half, width = q_in.shape[1:]
    tok = PARTS * half
    heads = width // HD
    a_width = A_HEADS * HD
    cols = w_in.shape[1] // (NXL * NC)
    tile = NZ * half
    scale = LOG2E / math.sqrt(HD)
    copies = Copies(send_sem, recv_sem)
    start = copies.start
    on_a, on_b = pl.ds(0, a_width), pl.ds(a_width, width - a_width)

    seq, head = lax.axis_index("seq"), lax.axis_index("head")
    y, xh, z = seq // (NX * NZ), (seq // NZ) % NX, seq % NZ
    xl, core = head // NC, head % NC

    def at(y_, xh_, z_):
        return (y_ * (NX * NZ) + xh_ * NZ + z_, head)

    z_up, z_down = at(y, xh, (z + 1) % NZ), at(y, xh, (z + NZ - 1) % NZ)
    z_up2, z_down2 = at(y, xh, (z + 2) % NZ), at(y, xh, (z + NZ - 2) % NZ)
    y_up, y_down = at((y + 1) % NY, xh, z), at((y + NY - 1) % NY, xh, z)
    x_far = at(y, 1 - xh, z)
    other_core = (seq, xl * NC + 1 - core)
    other_chip = (seq, (1 - xl) * NC + core)

    def qa_rows(slot):
        return pl.ds(ORDER.index(slot) * half, half)

    def qa_at(slot):
        return qa.at[:, qa_rows(slot), :]

    def a_at(ref, far, step):
        return ref.at[far, pl.ds(step * tok, tok), :]

    def qb_rows(far, step):
        return pl.ds((far * NY + step) * half, half)

    def qb_at(far, step):
        return qb.at[:, qb_rows(far, step), :]

    def b_at(ref, slot):
        return ref.at[pl.ds(slot * tok, tok), :]

    own = [
        pltpu.make_async_copy(q_in.at[:, :, on_a], qa_at(0), local_sem.at[0]),
        pltpu.make_async_copy(k_in.at[:, on_a], a_at(ka, 0, 0), local_sem.at[1]),
        pltpu.make_async_copy(v_in.at[:, on_a], a_at(va, 0, 0), local_sem.at[2]),
        pltpu.make_async_copy(q_in.at[:, :, on_b], qb_at(0, 0), local_sem.at[3]),
        pltpu.make_async_copy(k_in.at[:, on_b], b_at(kb, 0), local_sem.at[4]),
        pltpu.make_async_copy(v_in.at[:, on_b], b_at(vb, 0), local_sem.at[5]),
    ]
    my_rows = pl.ds(pl.multiple_of(core * width, width), width)
    their_rows = pl.ds(pl.multiple_of((1 - core) * width, width), width)

    def w_columns(x, c):
        return w_in.at[:, pl.ds(pl.multiple_of((x * NC + c) * cols, cols), cols)]

    weights = [
        pltpu.make_async_copy(w_columns(x, core), w_all.at[x, my_rows, :], local_sem.at[6 + x])
        for x in range(NXL)
    ]
    for copy in own:
        copy.start()
    for copy in weights:
        copy.start()

    partners = [z_up, z_down, z_up2, z_down2, other_core, other_chip]
    partners += [
        at((y + step) % NY, 1 - xh if x else xh, z)
        for x in range(NX)
        for step in range(NY)
        if x or step
    ]
    barrier = pltpu.get_barrier_semaphore()
    for partner in partners:
        pl.semaphore_signal(
            barrier, inc=1, device_id=partner, device_id_type=pl.DeviceIdType.MESH
        )
    stat_a[...] = jnp.zeros_like(stat_a)
    pst_a[...] = jnp.zeros_like(pst_a)
    pst_b[...] = jnp.zeros_like(pst_b)
    for copy in own:
        copy.wait()
    pl.semaphore_wait(barrier, len(partners))

    def attend(q, k):
        s = lax.dot_general(k, q, (((1,), (1,)), ((), ())), preferred_element_type=F32)
        return s, jnp.max(s, axis=0, keepdims=True) * scale

    def weigh(s, top, v):
        expo = jnp.exp2(s * scale - top)
        o = lax.dot_general(
            v, expo.astype(BF16), (((0,), (0,)), ((), ())), preferred_element_type=F32
        )
        return jnp.sum(expo, axis=0, keepdims=True), o

    def attend_a(r, lo, hi, far):
        for a in range(lo, hi, LANES):
            here = slice(r * tile + a, r * tile + a + LANES)
            for h in range(A_HEADS):
                hs = slice(h * HD, (h + 1) * HD)
                s, top = attend(qa[r, a : a + LANES, hs], ka[far, :, hs])
                if far:
                    before = stat_a[h : h + 1, here]
                    top = jnp.maximum(top, before)
                total, o = weigh(s, top, va[far, :, hs])
                if far:
                    kept = jnp.exp2(before - top)
                    total += kept * stat_a[8 + h : 9 + h, here]
                    o += kept * acc[hs, here]
                    part_a[r, a : a + LANES, hs] = jnp.transpose(o).astype(BF16)
                else:
                    acc[hs, here] = o
                stat_a[h : h + 1, here] = top
                stat_a[8 + h : 9 + h, here] = total
        if far:
            both = stat_a[:, r * tile : (r + 1) * tile]
            for n, slot in enumerate(ORDER):
                pst_a[r, slot, :, :half] = both[:, n * half : (n + 1) * half]

    def attend_b(r, h):
        hs = slice(h * HD, (h + 1) * HD)
        s, top = attend(qb[r, :, hs], kb[:, hs])
        total, o = weigh(s, top, vb[:, hs])
        o = jnp.transpose(o).astype(BF16)
        for n in range(NX * NY):
            here = slice(n * half, (n + 1) * half)
            part_b[r, n, :, hs] = o[here, :]
            pst_b[r, n, h : h + 1, :half] = top[:, here]
            pst_b[r, n, 8 + h : 9 + h, :half] = total[:, here]

    def long_a(r, d):
        return (NZ - d) % NZ if r else d

    def short_a(r, d):
        return d if r else (NZ - d) % NZ

    def send_a(n, r, slot, device):
        return (
            start(part_a.at[r, qa_rows(slot), :], got_a.at[r, n], device),
            start(pst_a.at[r, slot], gst_a.at[r, n], device),
        )

    def pass_on_a(n, r, slot, arrivals, device):
        o, stat = combine(
            [pst_a[r, slot]] + [gst_a[r, m] for m in arrivals],
            [part_a[r, qa_rows(slot), :]] + [got_a[r, m] for m in arrivals],
            A_HEADS,
            False,
        )
        part_a[r, qa_rows(slot), :] = o
        pst_a[r, slot] = stat
        return send_a(n, r, slot, device)

    longs_a, shorts_a, ends_a, spread_b = {}, {}, {}, {}

    def ring(r, step):
        far, near = (z_down, z_up) if r else (z_up, z_down)
        far2, near2 = (z_down2, z_up2) if r else (z_up2, z_down2)
        if step == 0:
            longs_a[r] = send_a(0, r, long_a(r, 4), far2) + send_a(1, r, long_a(r, 3), far)
            shorts_a[r] = send_a(2, r, short_a(r, 3), near)
            ends_a[r] = send_a(3, r, long_a(r, 1), far) + send_a(4, r, short_a(r, 1), near)
        else:
            arrive(*longs_a[r])
            longs_a[r] = pass_on_a(5, r, long_a(r, 2), (0, 1), far2)
            arrive(*shorts_a[r])
            shorts_a[r] = pass_on_a(6, r, short_a(r, 2), (2,), near2)

    def plane(r):
        spread_b[r] = []
        for step in (2, 1, 3, 0):
            for x in (1, 0):
                if x or step:
                    n = x * NY + step
                    owner = at((y + step) % NY, 1 - xh if x else xh, z)
                    spread_b[r] += [
                        start(part_b.at[r, n], got_b.at[r, n], owner),
                        start(pst_b.at[r, n], gst_b.at[r, n], owner),
                    ]

    def attended(r):
        arrive(*longs_a[r], *shorts_a[r], *ends_a[r], *spread_b[r])
        first = combine(
            [pst_a[r, 0]] + [gst_a[r, n] for n in range(3, 7)],
            [part_a[r, qa_rows(0), :]] + [got_a[r, n] for n in range(3, 7)],
            A_HEADS,
            True,
        )[0]
        second = combine(
            [pst_b[r, 0]] + [gst_b[r, n] for n in range(1, NX * NY)],
            [part_b[r, 0]] + [got_b[r, n] for n in range(1, NX * NY)],
            heads - A_HEADS,
            True,
        )[0]
        return jnp.concatenate([first, second], axis=1)

    def q_piece(r):
        return lambda slot: qa.at[r, qa_rows(slot), :]

    def kv_piece(ref):
        return lambda slot: b_at(ref, slot)

    q_streams = [(q_piece(0), True), (q_piece(1), False)]
    kv_streams = [(kv_piece(kb), True), (kv_piece(vb), False)]
    moving = {}

    def z_first(streams):
        for piece, up in streams:
            moving[piece] = [start(piece(0), piece(7), z_up), start(piece(0), piece(1), z_down)]

    def z_on(streams, d):
        for piece, up in streams:
            came_up, came_down = moving[piece]
            arrive(came_up)
            nxt = []
            if d < 3 or up:
                nxt.append(start(piece(8 - d), piece(7 - d), z_up))
            arrive(came_down)
            if d < 3 or not up:
                nxt.append(start(piece(d), piece(d + 1), z_down))
            moving[piece] = nxt

    def z_last(streams):
        for piece, up in streams:
            arrive(*moving[piece])

    z_first(q_streams)
    k_u = start(a_at(ka, 0, 0), a_at(ka, 0, 3), y_up)
    v_d = start(a_at(va, 0, 0), a_at(va, 0, 1), y_down)
    k_x = start(a_at(ka, 0, 0), a_at(ka, 1, 0), x_far)
    v_x = start(a_at(va, 0, 0), a_at(va, 1, 0), x_far)
    v_u = start(a_at(va, 0, 0), a_at(va, 0, 3), y_up)
    k_d = start(a_at(ka, 0, 0), a_at(ka, 0, 1), y_down)
    w_far = [
        start(w_columns(x, 1 - core), w_all.at[x, my_rows, :], other_core) for x in range(NXL)
    ]
    z_on(q_streams, 1)
    z_first(kv_streams)
    arrive(k_u)
    k_f = start(a_at(ka, 0, 3), a_at(ka, 0, 2), y_up)
    arrive(v_d)
    v_f = start(a_at(va, 0, 1), a_at(va, 0, 2), y_down)
    far_a = []
    for came, ref in ((k_x, ka), (v_x, va)):
        arrive(came)
        far_a += [
            start(a_at(ref, 1, 0), a_at(ref, 1, step), device)
            for step, device in ((3, y_up), (1, y_down))
        ]
    qb_x = start(qb_at(0, 0), qb_at(1, 0), x_far)
    z_on(q_streams, 2)
    z_on(kv_streams, 1)
    qb_u = start(qb_at(0, 0), qb_at(0, 3), y_up)
    qb_d = start(qb_at(0, 0), qb_at(0, 1), y_down)
    for came, ref in ((k_f, ka), (v_f, va)):
        arrive(came)
        far_a.append(start(a_at(ref, 0, 2), a_at(ref, 1, 2), x_far))
    arrive(qb_x)
    far_b = [
        start(qb_at(1, 0), qb_at(1, step), device) for step, device in ((3, y_up), (1, y_down))
    ]
    arrive(v_u, k_d)

    attend_a(0, 0, 384, 0)
    z_on(q_streams, 3)
    attend_a(1, 0, 384, 0)
    z_on(kv_streams, 2)
    attend_a(0, 384, 512, 0)
    attend_a(1, 384, 512, 0)
    arrive(qb_u)
    qb_u = start(qb.at[0, qb_rows(0, 3), :], qb.at[0, qb_rows(0, 2), :], y_up)
    arrive(qb_d)
    qb_d = start(qb.at[1, qb_rows(0, 1), :], qb.at[1, qb_rows(0, 2), :], y_down)
    z_last(q_streams)
    attend_a(0, 512, tile, 0)
    attend_a(1, 512, tile, 0)
    arrive(*far_a)
    z_on(kv_streams, 3)
    arrive(qb_u, qb_d)
    far_b.append(start(qb_at(0, 2), qb_at(1, 2), x_far))
    attend_a(0, 0, tile, 1)
    ring(0, 0)
    attend_a(1, 0, tile, 1)
    ring(1, 0)
    z_last(kv_streams)
    arrive(*far_b)
    for h in range(heads - A_HEADS):
        attend_b(0, h)
    plane(0)
    ring(0, 1)
    for h in range(heads - A_HEADS):
        attend_b(1, h)
    plane(1)
    ring(1, 1)

    for copy in weights:
        copy.wait()
    arrive(*w_far)

    def product(r, x):
        return sum(
            jnp.dot(
                att[r, c],
                w_all[x, c * width : (c + 1) * width, :],
                preferred_element_type=F32,
            )
            for c in range(NC)
        )

    sums = []
    piece = cols // 2
    for r in range(PARTS):
        att[r, core] = attended(r)
        swap = start(att.at[r, core], att.at[r, core], other_core)
        share = jnp.dot(att[r, core], w_all[1 - xl, my_rows, :], preferred_element_type=F32)
        arrive(swap)
        for n in range(2):
            cs = slice(n * piece, (n + 1) * piece)
            rest = jnp.dot(
                att[r, 1 - core], w_all[1 - xl, their_rows, cs], preferred_element_type=F32
            )
            term[r, n] = (share[:, cs] + rest).astype(BF16)
            sums.append(start(term.at[r, n], far_got.at[r, n], other_chip))
    for r in range(PARTS):
        mine[r] = product(r, xl)
    for r in range(PARTS):
        for n in range(2):
            cs = slice(n * piece, (n + 1) * piece)
            arrive(sums[2 * r + n])
            out_ref[r * half : (r + 1) * half, cs] = (
                mine[r, :, cs] + far_got[r, n].astype(F32)
            ).astype(BF16)
    for copy in copies.made:
        copy.wait_send()


def on_device(queries, keys, values, out_weight):
    tok, width = queries.shape
    depth = out_weight.shape[1]
    cols = depth // (NXL * NC)
    half = tok // PARTS
    a_width = A_HEADS * HD
    b_width = width - a_width
    anywhere = pl.BlockSpec(memory_space=pl.ANY)
    return pl.pallas_call(
        kernel,
        out_shape=jax.ShapeDtypeStruct((tok, cols), BF16),
        in_specs=[anywhere] * 4,
        out_specs=pl.BlockSpec(memory_space=pltpu.VMEM),
        scratch_shapes=[
            pltpu.VMEM((PARTS, NZ * half, a_width), BF16),
            pltpu.VMEM((NX, NY * tok, a_width), BF16),
            pltpu.VMEM((NX, NY * tok, a_width), BF16),
            pltpu.VMEM((PARTS, NX * NY * half, b_width), BF16),
            pltpu.VMEM((NZ * tok, b_width), BF16),
            pltpu.VMEM((NZ * tok, b_width), BF16),
            pltpu.VMEM((NXL, NC * width, cols), BF16),
            pltpu.VMEM((a_width, NZ * tok), F32),
            pltpu.VMEM((16, NZ * tok), F32),
            pltpu.VMEM((PARTS, NZ * half, a_width), BF16),
            pltpu.VMEM((PARTS, NZ, 16, HD), F32),
            pltpu.VMEM((PARTS, NZ - 1, half, a_width), BF16),
            pltpu.VMEM((PARTS, NZ - 1, 16, HD), F32),
            pltpu.VMEM((PARTS, NX * NY, half, b_width), BF16),
            pltpu.VMEM((PARTS, NX * NY, 16, HD), F32),
            pltpu.VMEM((PARTS, NX * NY, half, b_width), BF16),
            pltpu.VMEM((PARTS, NX * NY, 16, HD), F32),
            pltpu.VMEM((PARTS, NC, half, width), BF16),
            pltpu.VMEM((PARTS, 2, half, cols // 2), BF16),
            pltpu.VMEM((PARTS, 2, half, cols // 2), BF16),
            pltpu.VMEM((PARTS, half, cols), F32),
            pltpu.SemaphoreType.DMA((128,)),
            pltpu.SemaphoreType.DMA((128,)),
            pltpu.SemaphoreType.DMA((8,)),
        ],
        compiler_params=pltpu.CompilerParams(
            collective_id=0, has_side_effects=True, vmem_limit_bytes=56 << 20
        ),
    )(queries.reshape(PARTS, half, width), keys, values, out_weight)


def solution(mesh):
    placed = (P("seq", "head"), P("seq", "head"), P("seq", "head"), P("head", None))
    return jax.shard_map(
        on_device, mesh=mesh, in_specs=placed, out_specs=P("seq", "head"), check_vma=False
    )
```
